128 devices in a mesh: dp: 8 (over z_lo, x), tensor: 16 (over z_hi, y, core).
Axes of the slice: x: 4, y: 4, z: 4 (z_hi: 2, z_lo: 2; z = z_hi * 2 + z_lo), core: 2. Of those that a mesh axis runs over, the one named last changes fastest.
Arguments:
- saved_inputs: bfloat16 [3072, 6144], P(('dp', 'tensor')), may hold values from -24 to 24
- hidden_grads: bfloat16 [3072, 24576], P('dp', 'tensor'), may hold values from -6 to 6
- up_weight: bfloat16 [6144, 24576], P(None, 'tensor'), may hold values from -0.078125 to 0.078125
- up_bias: float32 [24576], P('tensor'), may hold values from -1 to 1
Outputs:
- input_grads: bfloat16 [3072, 6144], P(('dp', 'tensor'))
- weight_grads: bfloat16 [6144, 24576], P('dp', 'tensor')
The draws below stay inside these ranges and needn't reach their ends.
All inputs are finite; a program needn't handle non-finite values.
Results may differ from the reference program's by a relative error of at most 0.014.
Values may be sent and summed in bfloat16 or wider, within the bound.
A program may use at most 128 MiB of HBM per device.

```python
import jax
import jax.numpy as jnp
from jax import lax

D = 6144
FF = 24576
TOK_DEV = 384
TOKENS = 3072
N_DP = 8


def spiked(result, own_key, source, target, blocks, factor):
    def block_of(position):
        return (jnp.arange(result.shape[position]) // (result.shape[position] // blocks)).reshape((-1,) + (1,) * (result.ndim - 1 - position))

    near = jax.random.permutation(own_key, blocks)[block_of(target)]
    far = (block_of(target) + blocks // 2) % blocks
    return jnp.where((block_of(source) == near) | (block_of(source) == far), factor * result, result)


def levels(stream_key, dims, cuts, smallest, top_value):
    gain = 1.0
    for position, shards_of in cuts:
        steps = jax.random.uniform(jax.random.fold_in(jax.random.fold_in(stream_key, 6), position), (shards_of,), jnp.float32, smallest / len(cuts), top_value / len(cuts))
        gain = gain * jnp.repeat(jnp.exp(steps), dims[position] // shards_of).reshape((-1,) + (1,) * (len(dims) - 1 - position))
    return gain


def centred(rng, shape, deviation, limit, cuts=(), held_as=jnp.bfloat16):
    loudness = levels(rng, shape, cuts, -0.22, 0.18) if cuts else 1.0
    values = jax.random.normal(rng, shape, jnp.float32) * deviation * loudness
    return jnp.minimum(jnp.maximum(values, -limit), limit).astype(held_as)


def heavy_noise(key, dims, width, bound, cuts, heavy, kind=jnp.bfloat16):
    drawn = width * jax.random.normal(key, dims, jnp.float32)
    if cuts:
        drawn = drawn * levels(key, dims, cuts, -0.22, 0.18)
    return jnp.clip(spiked(drawn, jax.random.fold_in(key, 3), *heavy), -bound, bound).astype(kind)


def setup_inputs(seed: int = 0) -> dict:
    arg_keys = jax.random.split(jax.random.key(seed), 5)
    saved_inputs = heavy_noise(arg_keys[0], (TOKENS, D), 1.0, 24.0, ((0, 128),), (0, 1, 128, 5.5))
    hidden_grads = centred(arg_keys[1], (TOKENS, FF), 1.0, 6.0, ((0, 8), (1, 16)))
    up_weight = centred(arg_keys[2], (D, FF), D ** -0.5, 0.078125, ((1, 16),))
    up_bias = jnp.clip(jax.random.uniform(arg_keys[3], (FF,), jnp.float32, -1.0, 1.0) * levels(arg_keys[3], (FF,), ((0, 16),), -0.4, 0.0), -1.0, 1.0)
    return dict(saved_inputs=saved_inputs, hidden_grads=hidden_grads, up_weight=up_weight, up_bias=up_bias)


def slope(pre):
    cdf = 0.5 * (1.0 + jax.scipy.special.erf(pre * 0.7071067811865476))
    pdf = jnp.exp(-0.5 * pre * pre) * 0.3989422804014327
    return cdf + pre * pdf

def reference(saved_inputs, hidden_grads, up_weight, up_bias):
    pre = jnp.dot(saved_inputs, up_weight, preferred_element_type=jnp.float32) + up_bias.astype(jnp.float32)
    local_grads = (hidden_grads.astype(jnp.float32) * slope(pre)).astype(jnp.bfloat16)
    input_grads = lax.dot_general(local_grads, up_weight, (((1,), (1,)), ((), ())), preferred_element_type=jnp.float32).astype(jnp.bfloat16)
    inputs_rep = saved_inputs.reshape(N_DP, TOK_DEV, D)
    grads_rep = local_grads.reshape(N_DP, TOK_DEV, FF)

    def add_replica(total, pair):
        part = lax.dot_general(pair[0], pair[1], (((0,), (0,)), ((), ())), preferred_element_type=jnp.float32)
        rounded = lax.optimization_barrier(part.astype(jnp.bfloat16))
        return (total + rounded.astype(jnp.float32), None)
    summed, _ = lax.scan(add_replica, jnp.zeros((D, FF), jnp.float32), (inputs_rep, grads_rep))
    weight_grads = (summed * (1.0 / jnp.sqrt(jnp.float32(TOKENS)))).astype(jnp.bfloat16)
    return (input_grads, weight_grads)
```

```python
import functools

import jax
import jax.numpy as jnp
from jax import lax
from jax.experimental import pallas as pl
from jax.experimental.pallas import tpu as pltpu
from jax.sharding import PartitionSpec as P

MESH = pl.DeviceIdType.MESH
F32 = jnp.float32
BF16 = jnp.bfloat16

PIECES = 2
CHUNKS = 6

SWAP = 0
FIRST = 1
SECOND = FIRST + 17 * PIECES
EXCHANGE = SECOND + 17
GRADS = EXCHANGE + 4
HALVES = GRADS + 9 * CHUNKS
SCATTER = HALVES + CHUNKS
MESSAGES = SCATTER + 8


def slope(pre):
    cdf = 0.5 * (1.0 + lax.erf(pre * 0.7071067811865476))
    pdf = jnp.exp(-0.5 * pre * pre) * 0.3989422804014327
    return cdf + pre * pdf


class Gather:
    def __init__(self, post, await_, number, view, q, p, ring, pair, twin=None, mine=0, other=0):
        self.post, self.await_, self.number, self.view = post, await_, number, view
        self.q, self.p, self.ring, self.pair = q, p, ring, pair
        self.twin, self.mine, self.other = twin, mine, other

    def move(self, m, k, q, p, part, device):
        view = self.view(self.mine, q % 2, p % 4, part, k)
        self.post(self.number(m, k), view, view, device)

    def landed(self, m, k, q, p, part):
        self.await_(self.number(m, k), self.view(self.mine, q % 2, p % 4, part, k))

    def hand(self, m, k, q, p):
        if self.twin is not None:
            self.move(m, k, q, p, 2, self.twin)

    def own(self, k):
        q, p = self.q, self.p
        self.move(0, k, q, p, 2, self.pair)
        self.move(1, k, q, p, 2, self.ring(1))
        self.move(2, k, q, p, 2, self.ring(3))
        self.hand(9, k, q, p)

    def paired(self, k):
        q, p = self.q + 1, self.p
        self.landed(0, k, q, p, 2)
        self.move(3, k, q, p, 2, self.ring(1))
        self.move(4, k, q, p, 2, self.ring(3))
        self.hand(10, k, q, p)

    def halves(self, k, q, m, forward, hand):
        p = self.p
        self.landed(m, k, q, p + 3, 2)
        self.move(forward, k, q, p + 3, 0, self.ring(1))
        self.landed(m + 1, k, q, p + 1, 2)
        self.move(forward + 1, k, q, p + 1, 1, self.ring(3))
        self.hand(hand, k, q, p + 3)
        self.hand(hand + 1, k, q, p + 1)

    def near(self, k):
        self.halves(k, self.q, 1, 5, 11)

    def near_paired(self, k):
        self.halves(k, self.q + 1, 3, 7, 13)

    def far(self, k):
        self.landed(5, k, self.q, self.p + 2, 0)
        self.landed(6, k, self.q, self.p + 2, 1)
        self.hand(15, k, self.q, self.p + 2)

    def far_paired(self, k):
        self.landed(7, k, self.q + 1, self.p + 2, 0)
        self.landed(8, k, self.q + 1, self.p + 2, 1)
        self.hand(16, k, self.q + 1, self.p + 2)

    def handed(self, k):
        q, p = self.q, self.p
        places = ((q, p), (q + 1, p), (q, p + 3), (q, p + 1), (q + 1, p + 3), (q + 1, p + 1), (q, p + 2), (q + 1, p + 2))
        for i, (a, b) in enumerate(places):
            self.await_(self.number(9 + i, k), self.view(self.other, a % 2, b % 4, 2, k))

    def drain(self, drained, k):
        q, p = self.q, self.p
        parts = [2] * 5 + [0, 1, 0, 1] + ([2] * 8 if self.twin is not None else [])
        for m, part in enumerate(parts):
            drained(self.number(m, k), self.view(self.mine, q, p, part, k))


def kernel(
    factor, x_ref, hidden_hbm, weight_hbm, bias_ref, inputs_out, weights_out,
    weight, hidden, xr, xb, grads, partial, twin_part, near_part, next_part, pair_part, total, swap, share, final,
    sends, receives, loads,
):
    d, t = lax.axis_index("dp"), lax.axis_index("tensor")
    zl, x, zh, y, c = d // 4, d % 4, t // 8, (t // 2) % 4, t % 2
    o = 1 - c
    rows, model = x_ref.shape
    half = model // 2
    tokens, units = hidden.shape
    width = units // CHUNKS
    piece = half // PIECES
    block = model // 8
    step = half // CHUNKS

    def at(zl_, x_, zh_, y_, c_):
        return (zl_ * 4 + x_ % 4, zh_ * 8 + (y_ % 4) * 2 + c_)

    twin = at(zl, x, zh, y, o)
    pair_h = at(zl, x, 1 - zh, y, c)
    pair_l = at(1 - zl, x, zh, y, c)

    def ring_y(k):
        return at(zl, x, zh, y + k, c)

    def ring_x(k):
        return at(zl, x + k, zh, y, c)

    def post(m, src, dst, device):
        pltpu.make_async_remote_copy(
            src_ref=src, dst_ref=dst, send_sem=sends.at[m], recv_sem=receives.at[m], device_id=device, device_id_type=MESH
        ).start()

    def described(m, ref):
        return pltpu.make_async_remote_copy(
            src_ref=ref, dst_ref=ref, send_sem=sends.at[m], recv_sem=receives.at[m], device_id=twin, device_id_type=MESH
        )

    def landed(m, ref):
        described(m, ref).wait_recv()

    def drained(m, ref):
        described(m, ref).wait_send()

    def weight_load(j, h):
        part = pl.ds(h * half + j * piece, piece)
        return pltpu.make_async_copy(weight_hbm.at[part], weight.at[part], loads.at[2 * j + h])

    for j in range(PIECES):
        for h in range(2):
            weight_load(j, h).start()
    hidden_load = pltpu.make_async_copy(hidden_hbm, hidden, loads.at[2 * PIECES])
    hidden_load.start()

    barrier = pltpu.get_barrier_semaphore()
    greeted = [twin, pair_h, pair_l, ring_y(1), ring_y(3), ring_x(1), ring_x(3)]
    greeted += [at(o, x + k, zh, y, zl) for k in range(4)]
    for device in greeted:
        pl.semaphore_signal(barrier, inc=1, device_id=device, device_id_type=MESH)
    pl.semaphore_wait(barrier, len(greeted))

    own_half = pl.ds(pl.multiple_of(c * half, half), half)
    other_half = pl.ds(pl.multiple_of(o * half, half), half)
    post(SWAP, x_ref.at[:, other_half], swap, twin)
    mine = x_ref[:, own_half].astype(F32)
    landed(SWAP, swap)
    theirs = swap[...].astype(F32)
    upper = jnp.where(c == 0, mine, theirs)
    lower = jnp.where(c == 0, theirs, mine)
    xr[c, zh, y] = jnp.concatenate([upper, lower], axis=0).astype(BF16)

    def view_first(h, q, p, part, j):
        cols = (pl.ds(j * piece, piece // 2), pl.ds(j * piece + piece // 2, piece // 2), pl.ds(j * piece, piece))[part]
        return xr.at[h, q, p, :, cols]

    def view_second(h, q, p, part, j):
        return xb.at[h, q, p, (pl.ds(0, 2), pl.ds(2, 2), pl.ds(0, 4))[part]]

    def view_grads(h, q, p, part, k):
        near, all_ = tokens // 2, tokens
        lines = (pl.ds(0, near), pl.ds(near, near), pl.ds(0, all_))[part]
        return grads.at[q, p, lines, pl.ds(pl.multiple_of(k * width, width), width)]

    first = Gather(post, landed, lambda m, j: FIRST + 17 * j + m, view_first, zh, y, ring_y, pair_h, twin, c, o)
    second = Gather(post, landed, lambda m, j: SECOND + m, view_second, zh, y, ring_y, pair_h, twin, o, c)
    third = Gather(post, landed, lambda m, k: GRADS + CHUNKS * m + k, view_grads, zl, x, ring_x, pair_l)

    for j in range(PIECES):
        first.own(j)
    for k in range(4):
        cols = pl.ds(pl.multiple_of(((x + k) % 4) * block, block), block)
        post(EXCHANGE + k, xr.at[c, zh, y, :, cols], xb.at[zl, zh, y, x], at(c, x + k, zh, y, 1 - zl))

    for j in range(PIECES):
        first.paired(j)
    for j in range(PIECES):
        first.near(j)
    for k in range(4):
        landed(EXCHANGE + k, xb.at[o, zh, y, (x + 4 - k) % 4])

    def forward(j, n):
        cols = pl.ds(pl.multiple_of(n * width, width), width)
        out = None
        for h in range(2):
            a = xr[h, :, :, :, j * piece : (j + 1) * piece].reshape(tokens, piece)
            term = jnp.dot(a, weight[h * half + j * piece : h * half + (j + 1) * piece, cols], preferred_element_type=F32)
            out = term if out is None else out + term
        return out

    for j in range(PIECES):
        first.near_paired(j)
        first.far(j)
        first.far_paired(j)
        if j == PIECES - 1:
            second.own(0)
        first.handed(j)
        for h in range(2):
            weight_load(j, h).wait()
        if j < PIECES - 1:

            @pl.loop(0, CHUNKS)
            def _(n):
                cols = pl.ds(pl.multiple_of(n * width, width), width)
                if j == 0:
                    total[0:tokens, cols] = forward(j, n)
                else:
                    total[0:tokens, cols] += forward(j, n)

    hidden_load.wait()

    @pl.loop(0, CHUNKS)
    def _(n):
        cols = pl.ds(pl.multiple_of(n * width, width), width)
        pre = total[0:tokens, cols] + forward(PIECES - 1, n) + bias_ref[:, cols]
        total[0:tokens, cols] = pre
        strip = 32

        @pl.loop(0, tokens // strip)
        def _(s):
            lines = pl.ds(pl.multiple_of(s * strip, strip), strip)
            g = hidden[lines, cols].astype(F32) * slope(total[lines, cols])
            grads[zl, x, lines, cols] = g.astype(BF16)

        third.own(n)

    second.paired(0)
    second.near(0)

    def backward(h, n, w):
        lines = pl.ds(pl.multiple_of(h * half + n * w, w), w)
        return lax.dot_general(grads[zl, x], weight[lines, :], (((1,), (1,)), ((), ())), preferred_element_type=F32)

    narrow = step // 2

    def piece_of(n):
        return pl.ds(pl.multiple_of(n * narrow, narrow), narrow)

    def chunk_of(k):
        return pl.ds(pl.multiple_of(k * step, step), step)

    @pl.loop(0, CHUNKS)
    def _(k):
        third.paired(k)
        third.near(k)

        @pl.loop(0, 2)
        def _(i):
            n = 2 * k + i
            partial[o, :, :, :, piece_of(n)] = backward(o, n, narrow).astype(BF16).reshape(2, 4, 2 * rows, narrow)

        post(HALVES + k, partial.at[o, :, :, :, chunk_of(k)], twin_part.at[:, :, :, chunk_of(k)], twin)

    second.near_paired(0)
    second.far(0)

    @pl.loop(0, CHUNKS)
    def _(k):
        landed(HALVES + k, twin_part.at[:, :, :, chunk_of(k)])

        @pl.loop(0, 2)
        def _(i):
            n = 2 * k + i
            theirs = twin_part[:, :, :, piece_of(n)].reshape(tokens, narrow).astype(F32)
            partial[c, :, :, :, piece_of(n)] = (backward(c, n, narrow) + theirs).astype(BF16).reshape(2, 4, 2 * rows, narrow)

    left, right = pl.ds(0, half // 2), pl.ds(half // 2, half // 2)
    plus, minus, across = (y + 1) % 4, (y + 3) % 4, (y + 2) % 4

    post(SCATTER + 0, partial.at[c, :, across, :, left], near_part.at[0], ring_y(1))
    post(SCATTER + 1, partial.at[c, :, across, :, right], near_part.at[1], ring_y(3))
    post(SCATTER + 2, partial.at[c, :, plus, :, right], next_part.at[0, :, :, right], ring_y(1))
    post(SCATTER + 3, partial.at[c, :, minus, :, left], next_part.at[1, :, :, left], ring_y(3))
    second.far_paired(0)
    second.handed(0)

    def weight_term(q, p, cols):
        a = xb[q % 2, :, :, p % 4].reshape(tokens, block)
        g = grads[q % 2, p % 4, :, cols]
        return lax.dot_general(a, g, (((0,), (0,)), ((), ())), preferred_element_type=F32)

    def add_replica(q, p, start=False):
        @pl.loop(0, CHUNKS)
        def _(n):
            cols = pl.ds(pl.multiple_of(n * width, width), width)
            term = weight_term(q, p, cols)
            if start:
                total[:, cols] = term
            else:
                total[:, cols] += term

    add_replica(zl, x, True)
    third.near_paired(0)

    landed(SCATTER + 0, near_part.at[0])
    partial[c, :, plus, :, left] = (partial[c, :, plus, :, left].astype(F32) + near_part[0].astype(F32)).astype(BF16)
    post(SCATTER + 4, partial.at[c, :, plus, :, left], next_part.at[0, :, :, left], ring_y(1))
    landed(SCATTER + 1, near_part.at[1])
    partial[c, :, minus, :, right] = (partial[c, :, minus, :, right].astype(F32) + near_part[1].astype(F32)).astype(BF16)
    post(SCATTER + 5, partial.at[c, :, minus, :, right], next_part.at[1, :, :, right], ring_y(3))

    add_replica(zl + 1, x)
    third.near_paired(1)
    add_replica(zl, x + 3)
    third.near_paired(2)
    add_replica(zl, x + 1)

    landed(SCATTER + 2, next_part.at[0, :, :, right])
    landed(SCATTER + 3, next_part.at[1, :, :, left])
    landed(SCATTER + 4, next_part.at[0, :, :, left])
    landed(SCATTER + 5, next_part.at[1, :, :, right])

    def reduced(z):
        return partial[c, z, y].astype(F32) + next_part[0, z].astype(F32) + next_part[1, z].astype(F32)

    partial[c, 1 - zh, y] = reduced(1 - zh).astype(BF16)
    post(SCATTER + 6, partial.at[c, 1 - zh, y], pair_part, pair_h)

    @pl.loop(3, CHUNKS)
    def _(k):
        third.near_paired(k)

    landed(SCATTER + 6, pair_part)
    summed = reduced(zh) + pair_part[...].astype(F32)
    upper, lower = summed[0:rows], summed[rows : 2 * rows]
    share[...] = jnp.where(c == 0, lower, upper).astype(BF16)
    post(SCATTER + 7, share, final, twin)
    inputs_out[:, own_half] = jnp.where(c == 0, upper, lower).astype(BF16)

    add_replica(zl + 1, x + 3)
    add_replica(zl + 1, x + 1)
    landed(SCATTER + 7, final)
    inputs_out[:, other_half] = final[...]

    @pl.loop(0, CHUNKS)
    def _(k):
        third.far(k)

    add_replica(zl, x + 2)

    @pl.loop(0, CHUNKS)
    def _(k):
        third.far_paired(k)
        cols = pl.ds(pl.multiple_of(k * width, width), width)
        weights_out[:, cols] = ((total[:, cols] + weight_term(zl + 1, x + 2, cols)) * factor).astype(BF16)

    drained(SWAP, swap)
    for j in range(PIECES):
        first.drain(drained, j)
    second.drain(drained, 0)
    for k in range(4):
        drained(EXCHANGE + k, xb.at[zl, zh, y, x])

    @pl.loop(0, CHUNKS)
    def _(k):
        third.drain(drained, k)
        drained(HALVES + k, twin_part.at[:, :, :, chunk_of(k)])

    for m, ref in enumerate(
        [
            near_part.at[0], near_part.at[1], next_part.at[0, :, :, right], next_part.at[1, :, :, left],
            next_part.at[0, :, :, left], next_part.at[1, :, :, right], pair_part, share,
        ]
    ):
        drained(SCATTER + m, ref)


def body(saved_inputs, hidden_grads, up_weight, up_bias):
    rows, model = saved_inputs.shape
    tokens, units = hidden_grads.shape
    half, block = model // 2, model // 8
    factor = float(1.0 / (tokens * 8) ** 0.5)
    any_space, vmem = pl.BlockSpec(memory_space=pl.ANY), pl.BlockSpec(memory_space=pltpu.VMEM)
    return pl.pallas_call(
        functools.partial(kernel, factor),
        out_shape=(jax.ShapeDtypeStruct((rows, model), BF16), jax.ShapeDtypeStruct((block, units), BF16)),
        in_specs=[vmem, any_space, any_space, vmem],
        out_specs=(vmem, vmem),
        scratch_shapes=[
            pltpu.VMEM((model, units), BF16),
            pltpu.VMEM((tokens, units), BF16),
            pltpu.VMEM((2, 2, 4, 2 * rows, half), BF16),
            pltpu.VMEM((2, 2, 4, 4, 2 * rows, block), BF16),
            pltpu.VMEM((2, 4, tokens, units), BF16),
            pltpu.VMEM((2, 2, 4, 2 * rows, half), BF16),
            pltpu.VMEM((2, 4, 2 * rows, half), BF16),
            pltpu.VMEM((2, 2, 2 * rows, half // 2), BF16),
            pltpu.VMEM((2, 2, 2 * rows, half), BF16),
            pltpu.VMEM((2 * rows, half), BF16),
            pltpu.VMEM((block, units), F32),
            pltpu.VMEM((rows, half), BF16),
            pltpu.VMEM((rows, half), BF16),
            pltpu.VMEM((rows, half), BF16),
            pltpu.SemaphoreType.DMA((MESSAGES,)),
            pltpu.SemaphoreType.DMA((MESSAGES,)),
            pltpu.SemaphoreType.DMA((2 * PIECES + 1,)),
        ],
        compiler_params=pltpu.CompilerParams(collective_id=0, has_side_effects=True, vmem_limit_bytes=67043328),
        name="gelu_backward",
    )(saved_inputs, hidden_grads, up_weight, up_bias.reshape(1, -1))


def solution(mesh):
    return jax.shard_map(
        body,
        mesh=mesh,
        in_specs=(P(("dp", "tensor"), None), P("dp", "tensor"), P(None, "tensor"), P("tensor")),
        out_specs=(P(("dp", "tensor"), None), P("dp", "tensor")),
        check_vma=False,
    )
```

```python
import functools

import jax
import jax.numpy as jnp
from jax import lax
from jax.experimental import pallas as pl
from jax.experimental.pallas import tpu as pltpu
from jax.sharding import PartitionSpec as P

MESH = pl.DeviceIdType.MESH
F32 = jnp.float32
BF16 = jnp.bfloat16

PIECES = 2
CHUNKS = 6
OWN = CHUNKS
GROUP = CHUNKS // 2

SWAP = 0
FIRST = 1
SECOND = FIRST + 17 * PIECES
EXCHANGE = SECOND + 17
GRADS = EXCHANGE + 4
HALVES = GRADS + 9 * (CHUNKS + 1)
SCATTER = HALVES + 2 * GROUP
MESSAGES = SCATTER + 10


def slope(pre):
    cdf = 0.5 * (1.0 + lax.erf(pre * 0.7071067811865476))
    pdf = jnp.exp(-0.5 * pre * pre) * 0.3989422804014327
    return cdf + pre * pdf


class Gather:
    def __init__(self, post, await_, number, view, q, p, ring, pair, twin=None, mine=0, other=0, late=lambda k: False):
        self.post, self.await_, self.number, self.view = post, await_, number, view
        self.q, self.p, self.ring, self.pair = q, p, ring, pair
        self.twin, self.mine, self.other, self.late = twin, mine, other, late

    def places(self):
        q, p = self.q, self.p
        near = [(q, p), (q + 1, p), (q, p + 3), (q, p + 1)]
        return near + [(q + 1, p + 3), (q + 1, p + 1), (q, p + 2), (q + 1, p + 2)]

    def move(self, m, k, q, p, part, device):
        view = self.view(self.mine, q % 2, p % 4, part, k)
        self.post(self.number(m, k), view, view, device)

    def landed(self, m, k, q, p, part):
        self.await_(self.number(m, k), self.view(self.mine, q % 2, p % 4, part, k))

    def hand(self, m, k, q, p):
        if self.twin is not None:
            self.move(m, k, q, p, 2, self.twin)

    def either(self, k, late, early):
        (late if self.late(k) else early)()

    def own(self, k):
        q, p = self.q, self.p
        self.move(0, k, q, p, 2, self.pair)
        self.move(1, k, q, p, 2, self.ring(1))
        self.move(2, k, q, p, 2, self.ring(3))
        self.hand(9, k, q, p)

    def paired(self, k):
        q, p = self.q + 1, self.p
        self.landed(0, k, q, p, 2)

        def early():
            self.move(3, k, q, p, 2, self.ring(1))
            self.move(4, k, q, p, 2, self.ring(3))

        self.either(k, lambda: None, early)
        self.hand(10, k, q, p)

    def halves(self, k, q, m, forward):
        p = self.p
        self.landed(m, k, q, p + 3, 2)
        self.move(forward, k, q, p + 3, 0, self.ring(1))
        self.landed(m + 1, k, q, p + 1, 2)
        self.move(forward + 1, k, q, p + 1, 1, self.ring(3))

    def near(self, k):
        q, p = self.q, self.p
        self.halves(k, q, 1, 5)

        def late():
            self.move(3, k, q, p + 3, 2, self.pair)
            self.move(4, k, q, p + 1, 2, self.pair)

        self.either(k, late, lambda: None)
        self.hand(11, k, q, p + 3)
        self.hand(12, k, q, p + 1)

    def near_paired(self, k):
        q, p = self.q + 1, self.p

        def late():
            self.landed(3, k, q, p + 3, 2)
            self.landed(4, k, q, p + 1, 2)

        self.either(k, late, lambda: self.halves(k, q, 3, 7))
        self.hand(13, k, q, p + 3)
        self.hand(14, k, q, p + 1)

    def far(self, k):
        q, p = self.q, self.p + 2
        self.landed(5, k, q, p, 0)
        self.landed(6, k, q, p, 1)
        self.either(k, lambda: self.move(7, k, q, p, 2, self.pair), lambda: None)
        self.hand(15, k, q, p)

    def far_paired(self, k):
        q, p = self.q + 1, self.p + 2

        def early():
            self.landed(7, k, q, p, 0)
            self.landed(8, k, q, p, 1)

        self.either(k, lambda: self.landed(7, k, q, p, 2), early)
        self.hand(16, k, q, p)

    def handed(self, k, first=0, last=8):
        for i, (a, b) in list(enumerate(self.places()))[first:last]:
            self.await_(self.number(9 + i, k), self.view(self.other, a % 2, b % 4, 2, k))

    def drain(self, drained, k):
        def gone(m, part):
            drained(self.number(m, k), self.view(self.mine, self.q, self.p, part, k))

        def early():
            gone(7, 0)
            gone(8, 1)

        for m, part in enumerate([2] * 5 + [0, 1]):
            gone(m, part)
        self.either(k, lambda: gone(7, 2), early)
        if self.twin is not None:
            for m in range(9, 17):
                gone(m, 2)


def kernel(
    factor, x_ref, hidden_hbm, weight_hbm, bias_ref, inputs_hbm, weights_hbm,
    weight, hidden, xr, xb, xt, grads, outgoing, partial, twin_part, near_part, next_part, pair_part, total, swap, share, final,
    inputs_out, weights_out, sends, receives, loads, stores,
):
    d, t = lax.axis_index("dp"), lax.axis_index("tensor")
    zl, x, zh, y, c = d // 4, d % 4, t // 8, (t // 2) % 4, t % 2
    o = 1 - c
    rows, model = x_ref.shape
    half = model // 2
    tokens, units = hidden.shape
    width = units // GROUP
    lines = tokens // 2
    piece = half // PIECES
    block = model // 8
    step = half // GROUP

    def at(zl_, x_, zh_, y_, c_):
        return (zl_ * 4 + x_ % 4, zh_ * 8 + (y_ % 4) * 2 + c_)

    twin = at(zl, x, zh, y, o)
    pair_h = at(zl, x, 1 - zh, y, c)
    pair_l = at(1 - zl, x, zh, y, c)

    def ring_y(k):
        return at(zl, x, zh, y + k, c)

    def ring_x(k):
        return at(zl, x + k, zh, y, c)

    def post(m, src, dst, device):
        pltpu.make_async_remote_copy(
            src_ref=src, dst_ref=dst, send_sem=sends.at[m], recv_sem=receives.at[m], device_id=device, device_id_type=MESH
        ).start()

    def described(m, ref):
        return pltpu.make_async_remote_copy(
            src_ref=ref, dst_ref=ref, send_sem=sends.at[m], recv_sem=receives.at[m], device_id=twin, device_id_type=MESH
        )

    def landed(m, ref):
        described(m, ref).wait_recv()

    def drained(m, ref):
        described(m, ref).wait_send()

    def weight_load(j, h):
        part = pl.ds(h * half + j * piece, piece)
        return pltpu.make_async_copy(weight_hbm.at[part], weight.at[part], loads.at[2 * j + h])

    for j in range(PIECES):
        for h in range(2):
            weight_load(j, h).start()
    places = [(zh, y), (zh + 1, y), (zh, y + 3), (zh, y + 1), (zh + 1, y + 3), (zh + 1, y + 1), (zh, y + 2), (zh + 1, y + 2)]
    places = [(a % 2, b % 4) for a, b in places]
    hidden_loads = []
    for i, (a, b) in enumerate(places):
        source = pl.ds(pl.multiple_of((a * 4 + b) * (2 * rows), 2 * rows), 2 * rows)
        load = pltpu.make_async_copy(
            hidden_hbm.at[source], hidden.at[pl.ds(i * 2 * rows, 2 * rows)], loads.at[2 * PIECES + i]
        )
        load.start()
        hidden_loads.append(load)

    barrier = pltpu.get_barrier_semaphore()
    greeted = [twin, pair_h, pair_l, ring_y(1), ring_y(3), ring_x(1), ring_x(3)]
    greeted += [at(o, x + k, zh, y, zl) for k in range(4)]
    for device in greeted:
        pl.semaphore_signal(barrier, inc=1, device_id=device, device_id_type=MESH)
    pl.semaphore_wait(barrier, len(greeted))

    own_half = pl.ds(pl.multiple_of(c * half, half), half)
    other_half = pl.ds(pl.multiple_of(o * half, half), half)
    post(SWAP, x_ref.at[:, other_half], swap, twin)
    mine = x_ref[:, own_half].astype(F32)
    landed(SWAP, swap)
    theirs = swap[...].astype(F32)
    upper = jnp.where(c == 0, mine, theirs)
    lower = jnp.where(c == 0, theirs, mine)
    xr[c, zh, y] = jnp.concatenate([upper, lower], axis=0).astype(BF16)

    def late(k):
        return k % GROUP == 1 and k != OWN

    def view_first(h, q, p, part, j):
        cols = (pl.ds(j * piece, piece // 2), pl.ds(j * piece + piece // 2, piece // 2), pl.ds(j * piece, piece))[part]
        return xr.at[h, q, p, :, cols]

    def view_second(h, q, p, part, j):
        return xb.at[h, q, p, (pl.ds(0, 2), pl.ds(2, 2), pl.ds(0, 4))[part]]

    def view_grads(h, q, p, part, k):
        if k == OWN:
            start, stop, column, wide = 0, 2 * rows, 0, units
        else:
            start, stop = ((2 * rows, lines), (lines, tokens))[k // GROUP]
            column, wide = k % GROUP * width, width
        begin, size = ((0, wide // 2), (wide // 2, wide // 2), (0, wide))[part]
        return grads.at[q, p, pl.ds(start, stop - start), pl.ds(column + begin, size)]

    first = Gather(post, landed, lambda m, j: FIRST + 17 * j + m, view_first, zh, y, ring_y, pair_h, twin, c, o)
    second = Gather(post, landed, lambda m, j: SECOND + m, view_second, zh, y, ring_y, pair_h, twin, o, c)
    third = Gather(post, landed, lambda m, k: GRADS + (CHUNKS + 1) * m + k, view_grads, zl, x, ring_x, pair_l, late=late)

    for j in range(PIECES):
        first.own(j)

    for j in range(PIECES):
        first.handed(j, 0, 1)
    for j in range(PIECES):
        for h in range(2):
            weight_load(j, h).wait()
    for load in hidden_loads:
        load.wait()

    narrow = width // 2
    strip = 2 * rows

    def forward(start, stop, n):
        @pl.loop(2 * n, 2 * n + 2)
        def _(i):
            cols = pl.ds(pl.multiple_of(i * narrow, narrow), narrow)
            pre = bias_ref[cols].reshape(1, narrow)
            for h in range(2):
                a = jnp.concatenate([xr[h, a, b] for a, b in places[start:stop]], axis=0)
                pre = pre + jnp.dot(a, weight[h * half : (h + 1) * half, cols], preferred_element_type=F32)
            total[0 : (stop - start) * strip, 0:narrow] = pre

            @pl.loop(0, stop - start)
            def _(s):
                here = pl.ds(pl.multiple_of(s * strip, strip), strip)
                there = pl.ds(pl.multiple_of((start + s) * strip, strip), strip)
                g = hidden[there, cols].astype(F32) * slope(total[here, 0:narrow])
                grads[zl, x, there, cols] = g.astype(BF16)

    for n in range(GROUP):
        forward(0, 1, n)
    third.own(OWN)
    for j in range(PIECES):
        first.paired(j)
        first.near(j)
    for k in range(4):
        cols = pl.ds(pl.multiple_of(((x + k) % 4) * block, block), block)
        post(EXCHANGE + k, xr.at[c, zh, y, :, cols], xb.at[zl, zh, y, x], at(c, x + k, zh, y, 1 - zl))
    for j in range(PIECES):
        first.handed(j, 1, 4)

    thin = step // 4
    slots = (0, 1, 2, 4, 3, 5, 6, 7)

    def backward(h, group, n):
        part = pl.ds(pl.multiple_of(h * half + n * thin, thin), thin)
        g = grads[zl, x, group * lines : (group + 1) * lines, :]
        return lax.dot_general(g, weight[part, :], (((1,), (1,)), ((), ())), preferred_element_type=F32)

    def rows_of(group):
        return pl.ds(group * lines, lines)

    def piece_of(n):
        return pl.ds(pl.multiple_of(n * thin, thin), thin)

    def chunk_of(k):
        return pl.ds(pl.multiple_of(k * step, step), step)

    def backward_other(group, k):
        @pl.loop(4 * k, 4 * k + 4)
        def _(n):
            outgoing[rows_of(group), piece_of(n)] = backward(o, group, n).astype(BF16)

        here = (rows_of(group), chunk_of(k))
        post(HALVES + group * GROUP + k, outgoing.at[here], twin_part.at[here], twin)

    def backward_own(group, k):
        landed(HALVES + group * GROUP + k, twin_part.at[rows_of(group), chunk_of(k)])

        @pl.loop(4 * k, 4 * k + 4)
        def _(n):
            value = backward(c, group, n) + twin_part[rows_of(group), piece_of(n)].astype(F32)
            for i in range(4):
                partial[slots[4 * group + i], :, piece_of(n)] = value[i * 2 * rows : (i + 1) * 2 * rows].astype(BF16)

    near_replicas = [(zl, x), (zl + 1, x), (zl, x + 3), (zl, x + 1)]
    far_replicas = [(zl, x + 2), (zl + 1, x + 3), (zl + 1, x + 1), (zl + 1, x + 2)]

    def turn(replicas, group):
        for i, (q, p) in enumerate(replicas):
            some = places[4 * group : 4 * group + 4]
            block_rows = jnp.concatenate([xb[q % 2, a, b, p % 4] for a, b in some], axis=0)
            xt[:, i * lines : (i + 1) * lines] = block_rows.T

    def outer(replicas, group, n):
        cols = pl.ds(pl.multiple_of(n * narrow, narrow), narrow)
        g = jnp.concatenate([grads[q % 2, p % 4, group * lines : (group + 1) * lines, cols] for q, p in replicas], axis=0)
        return cols, jnp.dot(xt[...], g, preferred_element_type=F32)

    def add(replicas, group, start=False):
        turn(replicas, group)

        @pl.loop(0, 2 * GROUP)
        def _(n):
            cols, term = outer(replicas, group, n)
            if start:
                total[:, cols] = term
            else:
                total[:, cols] += term

    left, right = pl.ds(0, half // 2), pl.ds(half // 2, half // 2)
    minus, plus, across = pl.ds(2, 2), pl.ds(4, 2), pl.ds(6, 2)

    third.paired(OWN)
    third.near(OWN)
    forward(1, 4, 0)
    third.own(0)
    forward(1, 4, 1)
    third.own(1)
    first.near_paired(0)
    forward(1, 4, 2)
    third.own(2)
    for k in range(4):
        landed(EXCHANGE + k, xb.at[o, zh, y, (x + 4 - k) % 4])
    second.own(0)
    backward_other(0, 0)
    first.near_paired(1)
    backward_other(0, 1)
    third.paired(0)
    third.near(0)
    backward_other(0, 2)
    for j in range(PIECES):
        first.far(j)
    backward_own(0, 0)
    backward_own(0, 1)
    backward_own(0, 2)
    for j in range(PIECES):
        first.far_paired(j)
    third.near(1)
    third.paired(1)
    post(SCATTER + 2, partial.at[4, :, right], next_part.at[0, 0, :, right], ring_y(1))
    post(SCATTER + 3, partial.at[2, :, left], next_part.at[1, 0, :, left], ring_y(3))
    for j in range(PIECES):
        first.handed(j, 4, 8)
    forward(4, 8, 0)
    third.own(3)
    third.paired(2)
    third.near(2)
    forward(4, 8, 1)
    third.own(4)
    second.paired(0)
    second.near(0)
    forward(4, 8, 2)
    third.own(5)
    third.near_paired(0)
    third.near_paired(OWN)
    third.far(OWN)
    third.far(0)
    backward_other(1, 0)
    third.far(1)
    backward_other(1, 1)
    backward_other(1, 2)
    backward_own(1, 0)
    third.paired(3)
    third.near(3)
    backward_own(1, 1)
    backward_own(1, 2)

    post(SCATTER + 0, partial.at[across, :, left], near_part.at[0], ring_y(1))
    post(SCATTER + 1, partial.at[across, :, right], near_part.at[1], ring_y(3))
    second.near_paired(0)
    second.far(0)
    second.far_paired(0)
    third.near_paired(2)
    third.far(2)
    second.handed(0)
    add(near_replicas, 0, True)
    third.near(4)
    third.paired(4)
    landed(SCATTER + 0, near_part.at[0])
    partial[plus, :, left] = (partial[plus, :, left].astype(F32) + near_part[0].astype(F32)).astype(BF16)
    post(SCATTER + 4, partial.at[plus, :, left], next_part.at[0, :, :, left], ring_y(1))
    landed(SCATTER + 1, near_part.at[1])
    partial[minus, :, right] = (partial[minus, :, right].astype(F32) + near_part[1].astype(F32)).astype(BF16)
    post(SCATTER + 5, partial.at[minus, :, right], next_part.at[1, :, :, right], ring_y(3))
    post(SCATTER + 8, partial.at[5, :, right], next_part.at[0, 1, :, right], ring_y(1))
    post(SCATTER + 9, partial.at[3, :, left], next_part.at[1, 1, :, left], ring_y(3))
    third.paired(5)
    third.near(5)
    add(near_replicas, 1)
    third.near_paired(3)
    third.far(3)

    third.far(4)
    third.near_paired(1)
    landed(SCATTER + 2, next_part.at[0, 0, :, right])
    landed(SCATTER + 3, next_part.at[1, 0, :, left])
    landed(SCATTER + 8, next_part.at[0, 1, :, right])
    landed(SCATTER + 9, next_part.at[1, 1, :, left])
    landed(SCATTER + 4, next_part.at[0, :, :, left])
    landed(SCATTER + 5, next_part.at[1, :, :, right])

    def reduced(z):
        return partial[z].astype(F32) + next_part[0, z].astype(F32) + next_part[1, z].astype(F32)

    partial[1] = reduced(1).astype(BF16)
    post(SCATTER + 6, partial.at[1], pair_part, pair_h)

    third.near_paired(5)
    third.far_paired(OWN)
    third.far_paired(0)
    third.far_paired(1)
    third.far_paired(2)
    add(far_replicas, 0)
    third.far(5)
    landed(SCATTER + 6, pair_part)
    summed = reduced(0) + pair_part[...].astype(F32)
    upper, lower = summed[0:rows], summed[rows : 2 * rows]
    share[...] = jnp.where(c == 0, lower, upper).astype(BF16)
    post(SCATTER + 7, share, final, twin)
    inputs_out[:, own_half] = jnp.where(c == 0, upper, lower).astype(BF16)

    def weight_store(i):
        cols = pl.ds(pl.multiple_of(i * narrow, narrow), narrow)
        return pltpu.make_async_copy(weights_out.at[:, cols], weights_hbm.at[:, cols], stores.at[i])

    third.near_paired(4)
    turn(far_replicas, 1)

    for k in range(GROUP):
        third.far_paired(GROUP + k)

        @pl.loop(2 * k, 2 * k + 2)
        def _(n):
            cols, term = outer(far_replicas, 1, n)
            weights_out[:, cols] = ((total[:, cols] + term) * factor).astype(BF16)
            weight_store(n).start()

    landed(SCATTER + 7, final)
    inputs_out[:, other_half] = final[...]
    inputs_store = pltpu.make_async_copy(inputs_out, inputs_hbm, stores.at[2 * GROUP])
    inputs_store.start()


    @pl.loop(0, 2 * GROUP)
    def _(i):
        weight_store(i).wait()

    inputs_store.wait()
    drained(SWAP, swap)
    for j in range(PIECES):
        first.drain(drained, j)
    second.drain(drained, 0)
    for k in range(4):
        drained(EXCHANGE + k, xb.at[zl, zh, y, x])

    for k in range(CHUNKS + 1):
        third.drain(drained, k)
    for k in range(2 * GROUP):
        drained(HALVES + k, twin_part.at[rows_of(0), chunk_of(0)])

    for m, ref in enumerate(
        [
            near_part.at[0], near_part.at[1], next_part.at[0, 0, :, right], next_part.at[1, 0, :, left],
            next_part.at[0, :, :, left], next_part.at[1, :, :, right], pair_part, share,
            next_part.at[0, 1, :, right], next_part.at[1, 1, :, left],
        ]
    ):
        drained(SCATTER + m, ref)


def body(saved_inputs, hidden_grads, up_weight, up_bias):
    rows, model = saved_inputs.shape
    tokens, units = hidden_grads.shape
    half, block = model // 2, model // 8
    factor = float(1.0 / (tokens * 8) ** 0.5)
    any_space, vmem = pl.BlockSpec(memory_space=pl.ANY), pl.BlockSpec(memory_space=pltpu.VMEM)
    return pl.pallas_call(
        functools.partial(kernel, factor),
        out_shape=(jax.ShapeDtypeStruct((rows, model), BF16), jax.ShapeDtypeStruct((block, units), BF16)),
        in_specs=[vmem, any_space, any_space, vmem],
        out_specs=(any_space, any_space),
        scratch_shapes=[
            pltpu.VMEM((model, units), BF16),
            pltpu.VMEM((tokens, units), BF16),
            pltpu.VMEM((2, 2, 4, 2 * rows, half), BF16),
            pltpu.VMEM((2, 2, 4, 4, 2 * rows, block), BF16),
            pltpu.VMEM((block, 2 * tokens), BF16),
            pltpu.VMEM((2, 4, tokens, units), BF16),
            pltpu.VMEM((tokens, half), BF16),
            pltpu.VMEM((8, 2 * rows, half), BF16),
            pltpu.VMEM((tokens, half), BF16),
            pltpu.VMEM((2, 2, 2 * rows, half // 2), BF16),
            pltpu.VMEM((2, 2, 2 * rows, half), BF16),
            pltpu.VMEM((2 * rows, half), BF16),
            pltpu.VMEM((block, units), F32),
            pltpu.VMEM((rows, half), BF16),
            pltpu.VMEM((rows, half), BF16),
            pltpu.VMEM((rows, half), BF16),
            pltpu.VMEM((rows, model), BF16),
            pltpu.VMEM((block, units), BF16),
            pltpu.SemaphoreType.DMA((MESSAGES,)),
            pltpu.SemaphoreType.DMA((MESSAGES,)),
            pltpu.SemaphoreType.DMA((2 * PIECES + 8,)),
            pltpu.SemaphoreType.DMA((2 * GROUP + 1,)),
        ],
        compiler_params=pltpu.CompilerParams(collective_id=0, has_side_effects=True, vmem_limit_bytes=62000000),
        name="gelu_backward",
    )(saved_inputs, hidden_grads, up_weight, up_bias)


def solution(mesh):
    return jax.shard_map(
        body,
        mesh=mesh,
        in_specs=(P(("dp", "tensor"), None), P("dp", "tensor"), P(None, "tensor"), P("tensor")),
        out_specs=(P(("dp", "tensor"), None), P("dp", "tensor")),
        check_vma=False,
    )
```

```python
import functools

import jax
import jax.numpy as jnp
from jax import lax
from jax.experimental import pallas as pl
from jax.experimental.pallas import tpu as pltpu
from jax.sharding import PartitionSpec as P

MESH = pl.DeviceIdType.MESH
F32 = jnp.float32
BF16 = jnp.bfloat16

PIECES = 2
CHUNKS = 6
OWN = CHUNKS
GROUP = CHUNKS // 2

SWAP = 0
FIRST = 1
SECOND = FIRST + 17 * PIECES
EXCHANGE = SECOND + 17
GRADS = EXCHANGE + 4
HALVES = GRADS + 9 * (CHUNKS + 1)
SCATTER = HALVES + 2 * GROUP
MESSAGES = SCATTER + 10


def slope(pre):
    cdf = 0.5 * (1.0 + lax.erf(pre * 0.7071067811865476))
    pdf = jnp.exp(-0.5 * pre * pre) * 0.3989422804014327
    return cdf + pre * pdf


class Gather:
    def __init__(self, post, await_, number, view, q, p, ring, pair, twin=None, mine=0, other=0, late=lambda k: False):
        self.post, self.await_, self.number, self.view = post, await_, number, view
        self.q, self.p, self.ring, self.pair = q, p, ring, pair
        self.twin, self.mine, self.other, self.late = twin, mine, other, late

    def places(self):
        q, p = self.q, self.p
        near = [(q, p), (q + 1, p), (q, p + 3), (q, p + 1)]
        return near + [(q + 1, p + 3), (q + 1, p + 1), (q, p + 2), (q + 1, p + 2)]

    def move(self, m, k, q, p, part, device):
        view = self.view(self.mine, q % 2, p % 4, part, k)
        self.post(self.number(m, k), view, view, device)

    def landed(self, m, k, q, p, part):
        self.await_(self.number(m, k), self.view(self.mine, q % 2, p % 4, part, k))

    def hand(self, m, k, q, p):
        if self.twin is not None:
            self.move(m, k, q, p, 2, self.twin)

    def either(self, k, late, early):
        (late if self.late(k) else early)()

    def own(self, k):
        q, p = self.q, self.p
        self.move(0, k, q, p, 2, self.pair)
        self.move(1, k, q, p, 2, self.ring(1))
        self.move(2, k, q, p, 2, self.ring(3))
        self.hand(9, k, q, p)

    def paired(self, k):
        q, p = self.q + 1, self.p
        self.landed(0, k, q, p, 2)

        def early():
            self.move(3, k, q, p, 2, self.ring(1))
            self.move(4, k, q, p, 2, self.ring(3))

        self.either(k, lambda: None, early)
        self.hand(10, k, q, p)

    def halves(self, k, q, m, forward):
        p = self.p
        self.landed(m, k, q, p + 3, 2)
        self.move(forward, k, q, p + 3, 0, self.ring(1))
        self.landed(m + 1, k, q, p + 1, 2)
        self.move(forward + 1, k, q, p + 1, 1, self.ring(3))

    def near(self, k):
        q, p = self.q, self.p
        self.halves(k, q, 1, 5)

        def late():
            self.move(3, k, q, p + 3, 2, self.pair)
            self.move(4, k, q, p + 1, 2, self.pair)

        self.either(k, late, lambda: None)
        self.hand(11, k, q, p + 3)
        self.hand(12, k, q, p + 1)

    def near_paired(self, k):
        q, p = self.q + 1, self.p

        def late():
            self.landed(3, k, q, p + 3, 2)
            self.landed(4, k, q, p + 1, 2)

        self.either(k, late, lambda: self.halves(k, q, 3, 7))
        self.hand(13, k, q, p + 3)
        self.hand(14, k, q, p + 1)

    def far(self, k):
        q, p = self.q, self.p + 2
        self.landed(5, k, q, p, 0)
        self.landed(6, k, q, p, 1)
        self.either(k, lambda: self.move(7, k, q, p, 2, self.pair), lambda: None)
        self.hand(15, k, q, p)

    def far_paired(self, k):
        q, p = self.q + 1, self.p + 2

        def early():
            self.landed(7, k, q, p, 0)
            self.landed(8, k, q, p, 1)

        self.either(k, lambda: self.landed(7, k, q, p, 2), early)
        self.hand(16, k, q, p)

    def handed(self, k, first=0, last=8):
        for i, (a, b) in list(enumerate(self.places()))[first:last]:
            self.await_(self.number(9 + i, k), self.view(self.other, a % 2, b % 4, 2, k))

    def drain(self, drained, k):
        def gone(m, part):
            drained(self.number(m, k), self.view(self.mine, self.q, self.p, part, k))

        def early():
            gone(7, 0)
            gone(8, 1)

        for m, part in enumerate([2] * 5 + [0, 1]):
            gone(m, part)
        self.either(k, lambda: gone(7, 2), early)
        if self.twin is not None:
            for m in range(9, 17):
                gone(m, 2)


def kernel(
    factor, x_ref, hidden_hbm, weight_hbm, bias_ref, inputs_out, weights_out,
    weight, hidden, xr, xb, xt, grads, outgoing, partial, twin_part, near_part, next_part, pair_part, total, swap, share, final,
    sends, receives, loads,
):
    d, t = lax.axis_index("dp"), lax.axis_index("tensor")
    zl, x, zh, y, c = d // 4, d % 4, t // 8, (t // 2) % 4, t % 2
    o = 1 - c
    rows, model = x_ref.shape
    half = model // 2
    tokens, units = hidden.shape
    width = units // GROUP
    lines = tokens // 2
    piece = half // PIECES
    block = model // 8
    step = half // GROUP

    def at(zl_, x_, zh_, y_, c_):
        return (zl_ * 4 + x_ % 4, zh_ * 8 + (y_ % 4) * 2 + c_)

    twin = at(zl, x, zh, y, o)
    pair_h = at(zl, x, 1 - zh, y, c)
    pair_l = at(1 - zl, x, zh, y, c)

    def ring_y(k):
        return at(zl, x, zh, y + k, c)

    def ring_x(k):
        return at(zl, x + k, zh, y, c)

    def post(m, src, dst, device):
        pltpu.make_async_remote_copy(
            src_ref=src, dst_ref=dst, send_sem=sends.at[m], recv_sem=receives.at[m], device_id=device, device_id_type=MESH
        ).start()

    def described(m, ref):
        return pltpu.make_async_remote_copy(
            src_ref=ref, dst_ref=ref, send_sem=sends.at[m], recv_sem=receives.at[m], device_id=twin, device_id_type=MESH
        )

    def landed(m, ref):
        described(m, ref).wait_recv()

    def drained(m, ref):
        described(m, ref).wait_send()

    def weight_load(j, h):
        part = pl.ds(h * half + j * piece, piece)
        return pltpu.make_async_copy(weight_hbm.at[part], weight.at[part], loads.at[2 * j + h])

    for j in range(PIECES):
        for h in range(2):
            weight_load(j, h).start()
    places = [(zh, y), (zh + 1, y), (zh, y + 3), (zh, y + 1), (zh + 1, y + 3), (zh + 1, y + 1), (zh, y + 2), (zh + 1, y + 2)]
    places = [(a % 2, b % 4) for a, b in places]
    hidden_loads = []
    for i, (a, b) in enumerate(places):
        source = pl.ds(pl.multiple_of((a * 4 + b) * (2 * rows), 2 * rows), 2 * rows)
        load = pltpu.make_async_copy(
            hidden_hbm.at[source], hidden.at[pl.ds(i * 2 * rows, 2 * rows)], loads.at[2 * PIECES + i]
        )
        load.start()
        hidden_loads.append(load)

    barrier = pltpu.get_barrier_semaphore()
    greeted = [twin, pair_h, pair_l, ring_y(1), ring_y(3), ring_x(1), ring_x(3)]
    greeted += [at(o, x + k, zh, y, zl) for k in range(4)]
    for device in greeted:
        pl.semaphore_signal(barrier, inc=1, device_id=device, device_id_type=MESH)
    pl.semaphore_wait(barrier, len(greeted))

    own_half = pl.ds(pl.multiple_of(c * half, half), half)
    other_half = pl.ds(pl.multiple_of(o * half, half), half)
    post(SWAP, x_ref.at[:, other_half], swap, twin)
    mine = x_ref[:, own_half].astype(F32)
    landed(SWAP, swap)
    theirs = swap[...].astype(F32)
    upper = jnp.where(c == 0, mine, theirs)
    lower = jnp.where(c == 0, theirs, mine)
    xr[c, zh, y] = jnp.concatenate([upper, lower], axis=0).astype(BF16)

    def late(k):
        return k in (1, GROUP)

    def view_first(h, q, p, part, j):
        cols = (pl.ds(j * piece, piece // 2), pl.ds(j * piece + piece // 2, piece // 2), pl.ds(j * piece, piece))[part]
        return xr.at[h, q, p, :, cols]

    def view_second(h, q, p, part, j):
        return xb.at[h, q, p, (pl.ds(0, 2), pl.ds(2, 2), pl.ds(0, 4))[part]]

    def view_grads(h, q, p, part, k):
        if k == OWN:
            start, stop, column, wide = 0, 2 * rows, 0, units
        else:
            start, stop = ((2 * rows, lines), (lines, tokens))[k // GROUP]
            column, wide = k % GROUP * width, width
        begin, size = ((0, wide // 2), (wide // 2, wide // 2), (0, wide))[part]
        return grads.at[q, p, pl.ds(start, stop - start), pl.ds(column + begin, size)]

    first = Gather(post, landed, lambda m, j: FIRST + 17 * j + m, view_first, zh, y, ring_y, pair_h, twin, c, o)
    second = Gather(post, landed, lambda m, j: SECOND + m, view_second, zh, y, ring_y, pair_h, twin, o, c)
    third = Gather(post, landed, lambda m, k: GRADS + (CHUNKS + 1) * m + k, view_grads, zl, x, ring_x, pair_l, late=late)

    for j in range(PIECES):
        first.own(j)

    for j in range(PIECES):
        first.handed(j, 0, 1)
    for j in range(PIECES):
        for h in range(2):
            weight_load(j, h).wait()
    for load in hidden_loads:
        load.wait()

    narrow = width // 2
    strip = 2 * rows

    def forward(start, stop, n):
        @pl.loop(2 * n, 2 * n + 2)
        def _(i):
            cols = pl.ds(pl.multiple_of(i * narrow, narrow), narrow)
            pre = bias_ref[cols].reshape(1, narrow)
            for h in range(2):
                a = jnp.concatenate([xr[h, a, b] for a, b in places[start:stop]], axis=0)
                pre = pre + jnp.dot(a, weight[h * half : (h + 1) * half, cols], preferred_element_type=F32)
            total[0 : (stop - start) * strip, 0:narrow] = pre

            @pl.loop(0, stop - start)
            def _(s):
                here = pl.ds(pl.multiple_of(s * strip, strip), strip)
                there = pl.ds(pl.multiple_of((start + s) * strip, strip), strip)
                g = hidden[there, cols].astype(F32) * slope(total[here, 0:narrow])
                grads[zl, x, there, cols] = g.astype(BF16)

    for n in range(GROUP):
        forward(0, 1, n)
    third.own(OWN)
    for k in range(4):
        cols = pl.ds(pl.multiple_of(((x + k) % 4) * block, block), block)
        post(EXCHANGE + k, xr.at[c, zh, y, :, cols], xb.at[zl, zh, y, x], at(c, x + k, zh, y, 1 - zl))
    for j in range(PIECES):
        first.paired(j)
        first.near(j)
    for j in range(PIECES):
        first.handed(j, 1, 4)

    thin = step // 4
    slots = (0, 1, 2, 4, 3, 5, 6, 7)

    def backward(h, group, n):
        part = pl.ds(pl.multiple_of(h * half + n * thin, thin), thin)
        g = grads[zl, x, group * lines : (group + 1) * lines, :]
        return lax.dot_general(g, weight[part, :], (((1,), (1,)), ((), ())), preferred_element_type=F32)

    def rows_of(group):
        return pl.ds(group * lines, lines)

    def piece_of(n):
        return pl.ds(pl.multiple_of(n * thin, thin), thin)

    def chunk_of(k):
        return pl.ds(pl.multiple_of(k * step, step), step)

    def backward_other(group, k):
        @pl.loop(4 * k, 4 * k + 4)
        def _(n):
            outgoing[rows_of(group), piece_of(n)] = backward(o, group, n).astype(BF16)

        here = (rows_of(group), chunk_of(k))
        post(HALVES + group * GROUP + k, outgoing.at[here], twin_part.at[here], twin)

    def backward_own(group, k):
        landed(HALVES + group * GROUP + k, twin_part.at[rows_of(group), chunk_of(k)])

        @pl.loop(4 * k, 4 * k + 4)
        def _(n):
            value = backward(c, group, n) + twin_part[rows_of(group), piece_of(n)].astype(F32)
            for i in range(4):
                partial[slots[4 * group + i], :, piece_of(n)] = value[i * 2 * rows : (i + 1) * 2 * rows].astype(BF16)

    near_replicas = [(zl, x), (zl + 1, x), (zl, x + 3), (zl, x + 1)]
    far_replicas = [(zl, x + 2), (zl + 1, x + 3), (zl + 1, x + 1), (zl + 1, x + 2)]

    def turn(replicas, group):
        for i, (q, p) in enumerate(replicas):
            some = places[4 * group : 4 * group + 4]
            block_rows = jnp.concatenate([xb[q % 2, a, b, p % 4] for a, b in some], axis=0)
            xt[:, i * lines : (i + 1) * lines] = block_rows.T

    def outer(replicas, group, n):
        cols = pl.ds(pl.multiple_of(n * narrow, narrow), narrow)
        g = jnp.concatenate([grads[q % 2, p % 4, group * lines : (group + 1) * lines, cols] for q, p in replicas], axis=0)
        return cols, jnp.dot(xt[...], g, preferred_element_type=F32)

    def add(replicas, group, start=False):
        turn(replicas, group)

        @pl.loop(0, 2 * GROUP)
        def _(n):
            cols, term = outer(replicas, group, n)
            if start:
                total[:, cols] = term
            else:
                total[:, cols] += term

    left, right = pl.ds(0, half // 2), pl.ds(half // 2, half // 2)
    minus, plus, across = pl.ds(2, 2), pl.ds(4, 2), pl.ds(6, 2)

    third.paired(OWN)
    third.near(OWN)
    forward(1, 4, 0)
    third.own(0)
    forward(1, 4, 1)
    for k in range(4):
        landed(EXCHANGE + k, xb.at[o, zh, y, (x + 4 - k) % 4])
    second.own(0)
    third.own(1)
    first.near_paired(0)
    forward(1, 4, 2)
    third.own(2)
    backward_other(0, 0)
    first.near_paired(1)
    backward_other(0, 1)
    backward_other(0, 2)
    third.paired(0)
    third.near(0)
    for j in range(PIECES):
        first.far(j)
    backward_own(0, 0)
    backward_own(0, 1)
    backward_own(0, 2)
    third.near(1)
    third.paired(1)
    second.paired(0)
    second.near(0)
    for j in range(PIECES):
        first.far_paired(j)
    post(SCATTER + 2, partial.at[4, :, right], next_part.at[0, 0, :, right], ring_y(1))
    post(SCATTER + 3, partial.at[2, :, left], next_part.at[1, 0, :, left], ring_y(3))
    for j in range(PIECES):
        first.handed(j, 4, 8)
    forward(4, 8, 0)
    third.own(3)
    third.paired(2)
    third.near(2)
    forward(4, 8, 1)
    third.own(4)
    forward(4, 8, 2)
    third.own(5)
    third.near_paired(0)
    third.near_paired(OWN)
    third.far(OWN)
    third.far(0)
    backward_other(1, 0)
    third.far(1)
    second.near_paired(0)
    second.far(0)
    backward_other(1, 1)
    third.paired(3)
    third.near(3)
    backward_other(1, 2)
    backward_own(1, 0)
    second.far_paired(0)
    backward_own(1, 1)
    backward_own(1, 2)

    post(SCATTER + 0, partial.at[across, :, left], near_part.at[0], ring_y(1))
    post(SCATTER + 1, partial.at[across, :, right], near_part.at[1], ring_y(3))
    post(SCATTER + 8, partial.at[5, :, right], next_part.at[0, 1, :, right], ring_y(1))
    post(SCATTER + 9, partial.at[3, :, left], next_part.at[1, 1, :, left], ring_y(3))
    third.near_paired(2)
    third.far(2)
    second.handed(0)
    add(near_replicas, 0, True)
    third.near(4)
    third.paired(4)
    landed(SCATTER + 0, near_part.at[0])
    partial[plus, :, left] = (partial[plus, :, left].astype(F32) + near_part[0].astype(F32)).astype(BF16)
    post(SCATTER + 4, partial.at[plus, :, left], next_part.at[0, :, :, left], ring_y(1))
    landed(SCATTER + 1, near_part.at[1])
    partial[minus, :, right] = (partial[minus, :, right].astype(F32) + near_part[1].astype(F32)).astype(BF16)
    post(SCATTER + 5, partial.at[minus, :, right], next_part.at[1, :, :, right], ring_y(3))
    third.far(3)
    third.paired(5)
    third.near(5)
    add(near_replicas, 1)

    third.near_paired(4)
    third.near_paired(1)
    landed(SCATTER + 2, next_part.at[0, 0, :, right])
    landed(SCATTER + 3, next_part.at[1, 0, :, left])
    landed(SCATTER + 8, next_part.at[0, 1, :, right])
    landed(SCATTER + 9, next_part.at[1, 1, :, left])
    landed(SCATTER + 4, next_part.at[0, :, :, left])
    landed(SCATTER + 5, next_part.at[1, :, :, right])

    def reduced(z):
        return partial[z].astype(F32) + next_part[0, z].astype(F32) + next_part[1, z].astype(F32)

    partial[1] = reduced(1).astype(BF16)
    post(SCATTER + 6, partial.at[1], pair_part, pair_h)

    third.near_paired(5)
    third.far_paired(OWN)
    third.far_paired(0)
    third.far_paired(1)
    third.far_paired(2)
    add(far_replicas, 0)
    third.far(4)
    third.far(5)
    landed(SCATTER + 6, pair_part)
    summed = reduced(0) + pair_part[...].astype(F32)
    upper, lower = summed[0:rows], summed[rows : 2 * rows]
    share[...] = jnp.where(c == 0, lower, upper).astype(BF16)
    post(SCATTER + 7, share, final, twin)
    inputs_out[:, own_half] = jnp.where(c == 0, upper, lower).astype(BF16)

    third.near_paired(3)
    turn(far_replicas, 1)

    for k in range(GROUP):
        third.far_paired(GROUP + k)

        @pl.loop(2 * k, 2 * k + 2)
        def _(n):
            cols, term = outer(far_replicas, 1, n)
            weights_out[:, cols] = ((total[:, cols] + term) * factor).astype(BF16)

    landed(SCATTER + 7, final)
    inputs_out[:, other_half] = final[...]
    drained(SWAP, swap)
    for j in range(PIECES):
        first.drain(drained, j)
    second.drain(drained, 0)
    for k in range(4):
        drained(EXCHANGE + k, xb.at[zl, zh, y, x])

    for k in range(CHUNKS + 1):
        third.drain(drained, k)
    for k in range(2 * GROUP):
        drained(HALVES + k, twin_part.at[rows_of(0), chunk_of(0)])

    for m, ref in enumerate(
        [
            near_part.at[0], near_part.at[1], next_part.at[0, 0, :, right], next_part.at[1, 0, :, left],
            next_part.at[0, :, :, left], next_part.at[1, :, :, right], pair_part, share,
            next_part.at[0, 1, :, right], next_part.at[1, 1, :, left],
        ]
    ):
        drained(SCATTER + m, ref)


def body(saved_inputs, hidden_grads, up_weight, up_bias):
    rows, model = saved_inputs.shape
    tokens, units = hidden_grads.shape
    half, block = model // 2, model // 8
    factor = float(1.0 / (tokens * 8) ** 0.5)
    any_space, vmem = pl.BlockSpec(memory_space=pl.ANY), pl.BlockSpec(memory_space=pltpu.VMEM)
    return pl.pallas_call(
        functools.partial(kernel, factor),
        out_shape=(pltpu.VMEM((rows, model), BF16), pltpu.VMEM((block, units), BF16)),
        in_specs=[vmem, any_space, any_space, vmem],
        out_specs=(vmem, vmem),
        scratch_shapes=[
            pltpu.VMEM((model, units), BF16),
            pltpu.VMEM((tokens, units), BF16),
            pltpu.VMEM((2, 2, 4, 2 * rows, half), BF16),
            pltpu.VMEM((2, 2, 4, 4, 2 * rows, block), BF16),
            pltpu.VMEM((block, 2 * tokens), BF16),
            pltpu.VMEM((2, 4, tokens, units), BF16),
            pltpu.VMEM((tokens, half), BF16),
            pltpu.VMEM((8, 2 * rows, half), BF16),
            pltpu.VMEM((tokens, half), BF16),
            pltpu.VMEM((2, 2, 2 * rows, half // 2), BF16),
            pltpu.VMEM((2, 2, 2 * rows, half), BF16),
            pltpu.VMEM((2 * rows, half), BF16),
            pltpu.VMEM((block, units), F32),
            pltpu.VMEM((rows, half), BF16),
            pltpu.VMEM((rows, half), BF16),
            pltpu.VMEM((rows, half), BF16),
            pltpu.SemaphoreType.DMA((MESSAGES,)),
            pltpu.SemaphoreType.DMA((MESSAGES,)),
            pltpu.SemaphoreType.DMA((2 * PIECES + 8,)),
        ],
        compiler_params=pltpu.CompilerParams(collective_id=0, has_side_effects=True, vmem_limit_bytes=62000000),
        name="gelu_backward",
    )(saved_inputs, hidden_grads, up_weight, up_bias)


def solution(mesh):
    return jax.shard_map(
        body,
        mesh=mesh,
        in_specs=(P(("dp", "tensor"), None), P("dp", "tensor"), P(None, "tensor"), P("tensor")),
        out_specs=(P(("dp", "tensor"), None), P("dp", "tensor")),
        check_vma=False,
    )
```

```python
import functools

import jax
import jax.numpy as jnp
from jax import lax
from jax.experimental import pallas as pl
from jax.experimental.pallas import tpu as pltpu
from jax.sharding import PartitionSpec as P

MESH = pl.DeviceIdType.MESH
F32 = jnp.float32
BF16 = jnp.bfloat16

PIECES = 2
CHUNKS = 6
OWN = CHUNKS
GROUP = CHUNKS // 2

SWAP = 0
FIRST = 1
SECOND = FIRST + 17 * PIECES
EXCHANGE = SECOND + 17
GRADS = EXCHANGE + 4
HALVES = GRADS + 9 * (CHUNKS + 1)
SCATTER = HALVES + 2 * GROUP
MESSAGES = SCATTER + 14


def slope(pre):
    cdf = 0.5 * (1.0 + lax.erf(pre * 0.7071067811865476))
    pdf = jnp.exp(-0.5 * pre * pre) * 0.3989422804014327
    return cdf + pre * pdf


class Gather:
    def __init__(self, post, await_, number, view, q, p, ring, pair, twin=None, mine=0, other=0, late=lambda k: False):
        self.post, self.await_, self.number, self.view = post, await_, number, view
        self.q, self.p, self.ring, self.pair = q, p, ring, pair
        self.twin, self.mine, self.other, self.late = twin, mine, other, late

    def places(self):
        q, p = self.q, self.p
        near = [(q, p), (q + 1, p), (q, p + 3), (q, p + 1)]
        return near + [(q + 1, p + 3), (q + 1, p + 1), (q, p + 2), (q + 1, p + 2)]

    def move(self, m, k, q, p, part, device):
        view = self.view(self.mine, q % 2, p % 4, part, k)
        self.post(self.number(m, k), view, view, device)

    def landed(self, m, k, q, p, part):
        self.await_(self.number(m, k), self.view(self.mine, q % 2, p % 4, part, k))

    def hand(self, m, k, q, p):
        if self.twin is not None:
            self.move(m, k, q, p, 2, self.twin)

    def either(self, k, late, early):
        (late if self.late(k) else early)()

    def own(self, k):
        q, p = self.q, self.p
        self.move(0, k, q, p, 2, self.pair)
        self.move(1, k, q, p, 2, self.ring(1))
        self.move(2, k, q, p, 2, self.ring(3))
        self.hand(9, k, q, p)

    def paired(self, k):
        q, p = self.q + 1, self.p
        self.landed(0, k, q, p, 2)

        def early():
            self.move(3, k, q, p, 2, self.ring(1))
            self.move(4, k, q, p, 2, self.ring(3))

        self.either(k, lambda: None, early)
        self.hand(10, k, q, p)

    def halves(self, k, q, m, forward):
        p = self.p
        self.landed(m, k, q, p + 3, 2)
        self.move(forward, k, q, p + 3, 0, self.ring(1))
        self.landed(m + 1, k, q, p + 1, 2)
        self.move(forward + 1, k, q, p + 1, 1, self.ring(3))

    def near(self, k):
        q, p = self.q, self.p
        self.halves(k, q, 1, 5)

        def late():
            self.move(3, k, q, p + 3, 2, self.pair)
            self.move(4, k, q, p + 1, 2, self.pair)

        self.either(k, late, lambda: None)
        self.hand(11, k, q, p + 3)
        self.hand(12, k, q, p + 1)

    def near_paired(self, k):
        q, p = self.q + 1, self.p

        def late():
            self.landed(3, k, q, p + 3, 2)
            self.landed(4, k, q, p + 1, 2)

        self.either(k, late, lambda: self.halves(k, q, 3, 7))
        self.hand(13, k, q, p + 3)
        self.hand(14, k, q, p + 1)

    def far(self, k):
        q, p = self.q, self.p + 2
        self.landed(5, k, q, p, 0)
        self.landed(6, k, q, p, 1)
        self.either(k, lambda: self.move(7, k, q, p, 2, self.pair), lambda: None)
        self.hand(15, k, q, p)

    def far_paired(self, k):
        q, p = self.q + 1, self.p + 2

        def early():
            self.landed(7, k, q, p, 0)
            self.landed(8, k, q, p, 1)

        self.either(k, lambda: self.landed(7, k, q, p, 2), early)
        self.hand(16, k, q, p)

    def handed(self, k, first=0, last=8):
        for i, (a, b) in list(enumerate(self.places()))[first:last]:
            self.await_(self.number(9 + i, k), self.view(self.other, a % 2, b % 4, 2, k))

    def drain(self, drained, k):
        def gone(m, part):
            drained(self.number(m, k), self.view(self.mine, self.q, self.p, part, k))

        def early():
            gone(7, 0)
            gone(8, 1)

        for m, part in enumerate([2] * 5 + [0, 1]):
            gone(m, part)
        self.either(k, lambda: gone(7, 2), early)
        if self.twin is not None:
            for m in range(9, 17):
                gone(m, 2)


def kernel(
    factor, x_ref, hidden_hbm, weight_hbm, bias_ref, inputs_out, weights_out,
    weight, hidden, xr, xb, xt, grads, outgoing, partial, twin_part, near_part, next_part, pair_part, total, swap, share, final,
    sends, receives, loads,
):
    d, t = lax.axis_index("dp"), lax.axis_index("tensor")
    zl, x, zh, y, c = d // 4, d % 4, t // 8, (t // 2) % 4, t % 2
    o = 1 - c
    rows, model = x_ref.shape
    half = model // 2
    tokens, units = hidden.shape
    width = units // GROUP
    lines = tokens // 2
    piece = half // PIECES
    block = model // 8
    step = half // GROUP

    def at(zl_, x_, zh_, y_, c_):
        return (zl_ * 4 + x_ % 4, zh_ * 8 + (y_ % 4) * 2 + c_)

    twin = at(zl, x, zh, y, o)
    pair_h = at(zl, x, 1 - zh, y, c)
    pair_l = at(1 - zl, x, zh, y, c)

    def ring_y(k):
        return at(zl, x, zh, y + k, c)

    def ring_x(k):
        return at(zl, x + k, zh, y, c)

    def post(m, src, dst, device):
        pltpu.make_async_remote_copy(
            src_ref=src, dst_ref=dst, send_sem=sends.at[m], recv_sem=receives.at[m], device_id=device, device_id_type=MESH
        ).start()

    def described(m, ref):
        return pltpu.make_async_remote_copy(
            src_ref=ref, dst_ref=ref, send_sem=sends.at[m], recv_sem=receives.at[m], device_id=twin, device_id_type=MESH
        )

    def landed(m, ref):
        described(m, ref).wait_recv()

    def drained(m, ref):
        described(m, ref).wait_send()

    def weight_load(j, h):
        part = pl.ds(h * half + j * piece, piece)
        return pltpu.make_async_copy(weight_hbm.at[part], weight.at[part], loads.at[2 * j + h])

    for j in range(PIECES):
        for h in range(2):
            weight_load(j, h).start()
    places = [(zh, y), (zh + 1, y), (zh, y + 3), (zh, y + 1), (zh + 1, y + 3), (zh + 1, y + 1), (zh, y + 2), (zh + 1, y + 2)]
    places = [(a % 2, b % 4) for a, b in places]
    hidden_loads = []
    for i, (a, b) in enumerate(places):
        source = pl.ds(pl.multiple_of((a * 4 + b) * (2 * rows), 2 * rows), 2 * rows)
        load = pltpu.make_async_copy(
            hidden_hbm.at[source], hidden.at[pl.ds(i * 2 * rows, 2 * rows)], loads.at[2 * PIECES + i]
        )
        load.start()
        hidden_loads.append(load)

    barrier = pltpu.get_barrier_semaphore()
    greeted = [twin, pair_h, pair_l, ring_y(1), ring_y(3), ring_x(1), ring_x(3)]
    greeted += [at(o, x + k, zh, y, zl) for k in range(4)]
    for device in greeted:
        pl.semaphore_signal(barrier, inc=1, device_id=device, device_id_type=MESH)
    pl.semaphore_wait(barrier, len(greeted))

    own_half = pl.ds(pl.multiple_of(c * half, half), half)
    other_half = pl.ds(pl.multiple_of(o * half, half), half)
    post(SWAP, x_ref.at[:, other_half], swap, twin)
    mine = x_ref[:, own_half].astype(F32)
    landed(SWAP, swap)
    theirs = swap[...].astype(F32)
    upper = jnp.where(c == 0, mine, theirs)
    lower = jnp.where(c == 0, theirs, mine)
    xr[c, zh, y] = jnp.concatenate([upper, lower], axis=0).astype(BF16)

    def late(k):
        return k in (1, GROUP)

    def view_first(h, q, p, part, j):
        cols = (pl.ds(j * piece, piece // 2), pl.ds(j * piece + piece // 2, piece // 2), pl.ds(j * piece, piece))[part]
        return xr.at[h, q, p, :, cols]

    def view_second(h, q, p, part, j):
        return xb.at[h, q, p, (pl.ds(0, 2), pl.ds(2, 2), pl.ds(0, 4))[part]]

    def view_grads(h, q, p, part, k):
        if k == OWN:
            start, stop, column, wide = 0, 2 * rows, 0, units
        else:
            start, stop = ((2 * rows, lines), (lines, tokens))[k // GROUP]
            column, wide = k % GROUP * width, width
        begin, size = ((0, wide // 2), (wide // 2, wide // 2), (0, wide))[part]
        return grads.at[q, p, pl.ds(start, stop - start), pl.ds(column + begin, size)]

    first = Gather(post, landed, lambda m, j: FIRST + 17 * j + m, view_first, zh, y, ring_y, pair_h, twin, c, o)
    second = Gather(post, landed, lambda m, j: SECOND + m, view_second, zh, y, ring_y, pair_h, twin, o, c)
    third = Gather(post, landed, lambda m, k: GRADS + (CHUNKS + 1) * m + k, view_grads, zl, x, ring_x, pair_l, late=late)

    for j in range(PIECES):
        first.own(j)

    for j in range(PIECES):
        first.handed(j, 0, 1)
    for j in range(PIECES):
        for h in range(2):
            weight_load(j, h).wait()
    for load in hidden_loads:
        load.wait()

    narrow = width // 2
    strip = 2 * rows

    def forward(start, stop, n):
        @pl.loop(2 * n, 2 * n + 2)
        def _(i):
            cols = pl.ds(pl.multiple_of(i * narrow, narrow), narrow)
            pre = bias_ref[cols].reshape(1, narrow)
            for h in range(2):
                a = jnp.concatenate([xr[h, a, b] for a, b in places[start:stop]], axis=0)
                pre = pre + jnp.dot(a, weight[h * half : (h + 1) * half, cols], preferred_element_type=F32)
            total[0 : (stop - start) * strip, 0:narrow] = pre

            @pl.loop(0, stop - start)
            def _(s):
                here = pl.ds(pl.multiple_of(s * strip, strip), strip)
                there = pl.ds(pl.multiple_of((start + s) * strip, strip), strip)
                g = hidden[there, cols].astype(F32) * slope(total[here, 0:narrow])
                grads[zl, x, there, cols] = g.astype(BF16)

    for n in range(GROUP):
        forward(0, 1, n)
    third.own(OWN)
    for k in range(4):
        cols = pl.ds(pl.multiple_of(((x + k) % 4) * block, block), block)
        post(EXCHANGE + k, xr.at[c, zh, y, :, cols], xb.at[zl, zh, y, x], at(c, x + k, zh, y, 1 - zl))
    for j in range(PIECES):
        first.paired(j)
        first.near(j)
    for j in range(PIECES):
        first.handed(j, 1, 4)

    thin = step // 4
    slots = (0, 1, 2, 4, 3, 5, 6, 7)

    def backward(h, group, n):
        part = pl.ds(pl.multiple_of(h * half + n * thin, thin), thin)
        g = grads[zl, x, group * lines : (group + 1) * lines, :]
        return lax.dot_general(g, weight[part, :], (((1,), (1,)), ((), ())), preferred_element_type=F32)

    def rows_of(group):
        return pl.ds(group * lines, lines)

    def piece_of(n):
        return pl.ds(pl.multiple_of(n * thin, thin), thin)

    def chunk_of(k):
        return pl.ds(pl.multiple_of(k * step, step), step)

    def backward_other(group, k):
        @pl.loop(4 * k, 4 * k + 4)
        def _(n):
            outgoing[rows_of(group), piece_of(n)] = backward(o, group, n).astype(BF16)

        here = (rows_of(group), chunk_of(k))
        post(HALVES + group * GROUP + k, outgoing.at[here], twin_part.at[here], twin)

    def backward_own(group, k):
        landed(HALVES + group * GROUP + k, twin_part.at[rows_of(group), chunk_of(k)])

        @pl.loop(4 * k, 4 * k + 4)
        def _(n):
            value = backward(c, group, n) + twin_part[rows_of(group), piece_of(n)].astype(F32)
            for i in range(4):
                partial[slots[4 * group + i], :, piece_of(n)] = value[i * 2 * rows : (i + 1) * 2 * rows].astype(BF16)

    near_replicas = [(zl, x), (zl + 1, x), (zl, x + 3), (zl, x + 1)]
    far_replicas = [(zl, x + 2), (zl + 1, x + 3), (zl + 1, x + 1), (zl + 1, x + 2)]

    def turn(replicas, group):
        for i, (q, p) in enumerate(replicas):
            some = places[4 * group : 4 * group + 4]
            block_rows = jnp.concatenate([xb[q % 2, a, b, p % 4] for a, b in some], axis=0)
            xt[:, i * lines : (i + 1) * lines] = block_rows.T

    def outer(replicas, group, n):
        cols = pl.ds(pl.multiple_of(n * narrow, narrow), narrow)
        g = jnp.concatenate([grads[q % 2, p % 4, group * lines : (group + 1) * lines, cols] for q, p in replicas], axis=0)
        return cols, jnp.dot(xt[...], g, preferred_element_type=F32)

    def add(replicas, group, start=False):
        turn(replicas, group)

        @pl.loop(0, 2 * GROUP)
        def _(n):
            cols, term = outer(replicas, group, n)
            if start:
                total[:, cols] = term
            else:
                total[:, cols] += term

    left, right = pl.ds(0, half // 2), pl.ds(half // 2, half // 2)

    third.paired(OWN)
    third.near(OWN)
    forward(1, 4, 0)
    third.own(0)
    forward(1, 4, 1)
    for k in range(4):
        landed(EXCHANGE + k, xb.at[o, zh, y, (x + 4 - k) % 4])
    second.own(0)
    third.own(1)
    first.near_paired(0)
    forward(1, 4, 2)
    third.own(2)
    backward_other(0, 0)
    first.near_paired(1)
    backward_other(0, 1)
    backward_other(0, 2)
    third.paired(0)
    third.near(0)
    for j in range(PIECES):
        first.far(j)
    backward_own(0, 0)
    backward_own(0, 1)
    backward_own(0, 2)
    third.near(1)
    third.paired(1)
    second.paired(0)
    second.near(0)
    for j in range(PIECES):
        first.far_paired(j)
    post(SCATTER + 2, partial.at[4, :, right], next_part.at[0, 0, :, right], ring_y(1))
    post(SCATTER + 3, partial.at[2, :, left], next_part.at[1, 0, :, left], ring_y(3))
    for j in range(PIECES):
        first.handed(j, 4, 8)
    forward(4, 8, 0)
    third.own(3)
    third.paired(2)
    third.near(2)
    forward(4, 8, 1)
    third.own(4)
    forward(4, 8, 2)
    third.own(5)
    third.near_paired(0)
    third.near_paired(OWN)
    third.far(OWN)
    third.far(0)
    backward_other(1, 0)
    third.far(1)
    second.near_paired(0)
    second.far(0)
    backward_other(1, 1)
    third.paired(3)
    third.near(3)
    backward_other(1, 2)
    backward_own(1, 0)
    second.far_paired(0)
    backward_own(1, 1)
    backward_own(1, 2)

    post(SCATTER + 0, partial.at[7, :, left], near_part.at[0, 1], ring_y(1))
    post(SCATTER + 1, partial.at[7, :, right], near_part.at[1, 1], ring_y(3))
    post(SCATTER + 8, partial.at[5, :, right], next_part.at[0, 1, :, right], ring_y(1))
    post(SCATTER + 9, partial.at[3, :, left], next_part.at[1, 1, :, left], ring_y(3))
    post(SCATTER + 10, partial.at[6, :, left], near_part.at[0, 0], ring_y(1))
    post(SCATTER + 11, partial.at[6, :, right], near_part.at[1, 0], ring_y(3))
    third.near_paired(2)
    third.far(2)
    second.handed(0)
    add(near_replicas, 0, True)
    third.near(4)
    third.paired(4)
    third.paired(5)
    third.near(5)
    def pass_on(m, slot, side, i, z, device):
        landed(m, near_part.at[i, z])
        partial[slot, :, side] = (partial[slot, :, side].astype(F32) + near_part[i, z].astype(F32)).astype(BF16)
        post(m + 4 if z else m + 2, partial.at[slot, :, side], next_part.at[i, z, :, side], device)

    pass_on(SCATTER + 0, 5, left, 0, 1, ring_y(1))
    pass_on(SCATTER + 1, 3, right, 1, 1, ring_y(3))
    add(near_replicas, 1)
    third.far(3)
    pass_on(SCATTER + 10, 4, left, 0, 0, ring_y(1))
    pass_on(SCATTER + 11, 2, right, 1, 0, ring_y(3))

    landed(SCATTER + 8, next_part.at[0, 1, :, right])
    landed(SCATTER + 9, next_part.at[1, 1, :, left])
    landed(SCATTER + 4, next_part.at[0, 1, :, left])
    landed(SCATTER + 5, next_part.at[1, 1, :, right])

    def reduced(z):
        return partial[z].astype(F32) + next_part[0, z].astype(F32) + next_part[1, z].astype(F32)

    partial[1] = reduced(1).astype(BF16)
    post(SCATTER + 6, partial.at[1], pair_part, pair_h)

    third.near_paired(4)
    third.near_paired(1)
    third.far_paired(OWN)
    third.far_paired(0)
    third.far_paired(1)
    third.far_paired(2)
    add(far_replicas, 0)
    turn(far_replicas, 1)
    third.near_paired(5)
    third.far(4)
    third.far(5)
    landed(SCATTER + 2, next_part.at[0, 0, :, right])
    landed(SCATTER + 3, next_part.at[1, 0, :, left])
    landed(SCATTER + 12, next_part.at[0, 0, :, left])
    landed(SCATTER + 13, next_part.at[1, 0, :, right])
    landed(SCATTER + 6, pair_part)
    summed = reduced(0) + pair_part[...].astype(F32)
    upper, lower = summed[0:rows], summed[rows : 2 * rows]
    share[...] = jnp.where(c == 0, lower, upper).astype(BF16)
    post(SCATTER + 7, share, final, twin)
    inputs_out[:, own_half] = jnp.where(c == 0, upper, lower).astype(BF16)

    third.near_paired(3)

    for k in range(GROUP):
        third.far_paired(GROUP + k)

        @pl.loop(2 * k, 2 * k + 2)
        def _(n):
            cols, term = outer(far_replicas, 1, n)
            weights_out[:, cols] = ((total[:, cols] + term) * factor).astype(BF16)

    landed(SCATTER + 7, final)
    inputs_out[:, other_half] = final[...]
    drained(SWAP, swap)
    for j in range(PIECES):
        first.drain(drained, j)
    second.drain(drained, 0)
    for k in range(4):
        drained(EXCHANGE + k, xb.at[zl, zh, y, x])

    for k in range(CHUNKS + 1):
        third.drain(drained, k)
    for k in range(2 * GROUP):
        drained(HALVES + k, twin_part.at[rows_of(0), chunk_of(0)])

    for m, ref in enumerate(
        [
            near_part.at[0, 1], near_part.at[1, 1], next_part.at[0, 0, :, right], next_part.at[1, 0, :, left],
            next_part.at[0, 1, :, left], next_part.at[1, 1, :, right], pair_part, share,
            next_part.at[0, 1, :, right], next_part.at[1, 1, :, left], near_part.at[0, 0], near_part.at[1, 0],
            next_part.at[0, 0, :, left], next_part.at[1, 0, :, right],
        ]
    ):
        drained(SCATTER + m, ref)


def body(saved_inputs, hidden_grads, up_weight, up_bias):
    rows, model = saved_inputs.shape
    tokens, units = hidden_grads.shape
    half, block = model // 2, model // 8
    factor = float(1.0 / (tokens * 8) ** 0.5)
    any_space, vmem = pl.BlockSpec(memory_space=pl.ANY), pl.BlockSpec(memory_space=pltpu.VMEM)
    return pl.pallas_call(
        functools.partial(kernel, factor),
        out_shape=(pltpu.VMEM((rows, model), BF16), pltpu.VMEM((block, units), BF16)),
        in_specs=[vmem, any_space, any_space, vmem],
        out_specs=(vmem, vmem),
        scratch_shapes=[
            pltpu.VMEM((model, units), BF16),
            pltpu.VMEM((tokens, units), BF16),
            pltpu.VMEM((2, 2, 4, 2 * rows, half), BF16),
            pltpu.VMEM((2, 2, 4, 4, 2 * rows, block), BF16),
            pltpu.VMEM((block, 2 * tokens), BF16),
            pltpu.VMEM((2, 4, tokens, units), BF16),
            pltpu.VMEM((tokens, half), BF16),
            pltpu.VMEM((8, 2 * rows, half), BF16),
            pltpu.VMEM((tokens, half), BF16),
            pltpu.VMEM((2, 2, 2 * rows, half // 2), BF16),
            pltpu.VMEM((2, 2, 2 * rows, half), BF16),
            pltpu.VMEM((2 * rows, half), BF16),
            pltpu.VMEM((block, units), F32),
            pltpu.VMEM((rows, half), BF16),
            pltpu.VMEM((rows, half), BF16),
            pltpu.VMEM((rows, half), BF16),
            pltpu.SemaphoreType.DMA((MESSAGES,)),
            pltpu.SemaphoreType.DMA((MESSAGES,)),
            pltpu.SemaphoreType.DMA((2 * PIECES + 8,)),
        ],
        compiler_params=pltpu.CompilerParams(collective_id=0, has_side_effects=True, vmem_limit_bytes=62000000),
        name="gelu_backward",
    )(saved_inputs, hidden_grads, up_weight, up_bias)


def solution(mesh):
    return jax.shard_map(
        body,
        mesh=mesh,
        in_specs=(P(("dp", "tensor"), None), P("dp", "tensor"), P(None, "tensor"), P("tensor")),
        out_specs=(P(("dp", "tensor"), None), P("dp", "tensor")),
        check_vma=False,
    )
```
